256 devices in a mesh: wide: 64 (over x, z_lo, y, core), narrow: 4 (over z_hi).
Axes of the slice: x: 4, y: 4, z: 8 (z_hi: 4, z_lo: 2; z = z_hi * 2 + z_lo), core: 2. Of those that a mesh axis runs over, the one named last changes fastest.
Arguments:
- token_ids: int32 [128], P('wide'), may hold values from 0 to 65535
- attr_ids: int32 [128], replicated, may hold values from 0 to 65535
- target: int32 [128], P('wide'), may hold values from 0 to 127
- loss_mask: int32 [128], P('wide'), may hold values 0 or 1
- embed_table: bfloat16 [65536, 8192], P('wide', 'narrow'), may hold values from -30 to 30
- norm_gain: float32 [8192], P('narrow'), may hold values from 0.1 to 1.9
- w_gate: bfloat16 [8192, 28672], P('narrow', 'wide'), may hold values from -0.0625 to 0.0625
- w_up: bfloat16 [8192, 28672], P('narrow', 'wide'), may hold values from -0.0625 to 0.0625
- w_down: bfloat16 [28672, 8192], P('wide', 'narrow'), may hold values from -0.03125 to 0.03125
Outputs:
- grad_embed: bfloat16 [128, 8192], P('wide', 'narrow')
The draws below stay inside these ranges and needn't reach their ends.
All inputs are finite; a program needn't handle non-finite values. No bound on the sum of `loss_mask` on one device may be relied on, other than what follows from the above.
Results may differ from the reference program's by a relative error of at most 0.039.
Values may be sent and summed in bfloat16 or wider, within the bound.
No kernel may reach another device: no remote copies, remote signals or barrier semaphores. Data moves between devices by JAX's collectives and lax.ppermute only.
A program may use at most 64 MiB of HBM per device.

```python
import math
import jax
import jax.numpy as jnp
import numpy as np
from jax import lax

D = 8192
FF = 28672
ATTRS = 128
TOKENS = 128
VOCAB = 65536


def draw_embed_table(key, part):
    first, second, third = jax.random.split(key, 3)
    base = jnp.clip(jax.random.normal(first, (VOCAB, D), jnp.float32), -4.0, 4.0)
    column = jnp.exp(jax.random.uniform(second, (D,), jnp.float32, 0.0, math.log(10.0)))
    ramp = jnp.exp(jnp.arange(D, dtype=jnp.float32) * (math.log(3.0) / D))
    row_scale = jnp.exp(jax.random.uniform(third, (VOCAB, 1), jnp.float32, -0.69, 0.69))
    return (base * column * ramp * 0.11 * row_scale).astype(jnp.bfloat16)


def touch_ends(drawn, own_key, least, high):
    shape = drawn.shape
    spot = [jax.random.randint(jax.random.fold_in(own_key, axis), (), 0, shape[axis]) for axis in range(len(shape))]
    drawn = drawn.at[tuple(spot)].set(least)
    longest = shape.index(max(shape))
    spot[longest] = (spot[longest] + 1) % shape[longest]
    return drawn.at[tuple(spot)].set(high)


def levels(stream_key, dims, pieces, low, high):
    factor_of = 1.0
    for dim, shards_of in pieces:
        steps = jax.random.uniform(jax.random.fold_in(jax.random.fold_in(stream_key, 6), dim), (shards_of,), jnp.float32, low / len(pieces), high / len(pieces))
        factor_of = factor_of * jnp.repeat(jnp.exp(steps), dims[dim] // shards_of).reshape((-1,) + (1,) * (len(dims) - 1 - dim))
    return factor_of


def rank_bounds(count, skew):
    loads = [(1 << 20) // math.isqrt(standing ** skew) + 1 for standing in range(1, count + 1)]
    spread = 1 + sum(loads) // (1 << 30)
    return np.cumsum(np.array([max(1, weight // spread) for weight in loads]))


def ranked_ids(key, extent, number_of, skew):
    table = rank_bounds(number_of, skew)
    pick = jax.random.randint(jax.random.fold_in(key, 1), extent, 0, int(table[number_of - 1]))
    rank = jnp.searchsorted(jnp.asarray(table, jnp.int32), pick, side="right")
    return jax.random.permutation(jax.random.fold_in(key, 2), number_of)[rank].astype(jnp.int32)


def noise(rng, dims, deviation, limit, pieces=(), kind=jnp.bfloat16):
    entries = deviation * jax.random.normal(rng, dims, jnp.float32)
    if pieces:
        entries = entries * levels(rng, dims, pieces, -0.22, 0.18)
    return jnp.clip(entries, -limit, limit).astype(kind)


def setup_inputs(seed: int = 0) -> dict:
    key_of = jax.random.split(jax.random.key(seed), 10)
    return {
        "token_ids": touch_ends(ranked_ids(key_of[0], (TOKENS,), VOCAB, 2), jax.random.fold_in(key_of[0], 3), 0, VOCAB - 1).astype(jnp.int32),
        "attr_ids": touch_ends(jax.random.randint(key_of[1], (ATTRS,), 0, VOCAB), jax.random.fold_in(key_of[1], 1), 0, VOCAB - 1).astype(jnp.int32),
        "target": touch_ends(jax.random.randint(key_of[2], (TOKENS,), 0, ATTRS), jax.random.fold_in(key_of[2], 1), 0, ATTRS - 1).astype(jnp.int32),
        "loss_mask": touch_ends((jax.random.randint(key_of[3], (TOKENS,), 0, 4) < 3).astype(jnp.int32), jax.random.fold_in(key_of[3], 1), 0, 1),
        "embed_table": draw_embed_table(jax.random.fold_in(key_of[9], 71), 0),
        "norm_gain": jnp.clip(1.0 + 0.18 * jax.random.normal(key_of[5], (D,), jnp.float32), 0.1, 1.9),
        "w_gate": noise(key_of[6], (D, FF), D ** -0.5, 0.0625, ((0, 4), (1, 64))),
        "w_up": noise(key_of[7], (D, FF), D ** -0.5, 0.0625, ((0, 4), (1, 64))),
        "w_down": noise(key_of[8], (FF, D), FF ** -0.5, 0.03125, ((0, 64), (1, 4))),
    }


EPS = 1e-05

def reference(token_ids, attr_ids, target, loss_mask, embed_table, norm_gain, w_gate, w_up, w_down):
    embedded = jnp.take(embed_table, token_ids, axis=0)
    probe_rows = jnp.take(embed_table, attr_ids, axis=0)
    embed_rows = embedded.astype(jnp.float32)
    inv_rms = lax.rsqrt(lax.optimization_barrier(jnp.mean(embed_rows * embed_rows, axis=1, keepdims=True)) + EPS)
    normed = (embed_rows * inv_rms * norm_gain).astype(jnp.bfloat16)
    gate_pre = jnp.dot(normed, w_gate, preferred_element_type=jnp.float32)
    up_pre = jnp.dot(normed, w_up, preferred_element_type=jnp.float32)
    gate_sigmoid = jax.nn.sigmoid(gate_pre)
    hidden = (gate_pre * gate_sigmoid * up_pre).astype(jnp.bfloat16)
    block_out = embed_rows + jnp.dot(hidden, w_down, preferred_element_type=jnp.float32)
    logits = jnp.dot(block_out.astype(jnp.bfloat16), probe_rows.T, preferred_element_type=jnp.float32) * (3.0 / math.sqrt(D))
    probability = jax.nn.softmax(logits, axis=1)
    onehot = (target[:, None] == jnp.arange(ATTRS, dtype=jnp.int32)[None, :]).astype(jnp.float32)
    logit_grad = ((probability - onehot) * loss_mask[:, None].astype(jnp.float32)).astype(jnp.bfloat16)
    out_grad = jnp.dot(logit_grad, probe_rows, preferred_element_type=jnp.float32)
    hidden_grad = jnp.dot(out_grad.astype(jnp.bfloat16), w_down.T, preferred_element_type=jnp.float32)
    gate_grad = (hidden_grad * up_pre * gate_sigmoid * (1.0 + gate_pre * (1.0 - gate_sigmoid))).astype(jnp.bfloat16)
    up_grad = (hidden_grad * gate_pre * gate_sigmoid).astype(jnp.bfloat16)
    normed_grad = jnp.dot(gate_grad, w_gate.T, preferred_element_type=jnp.float32) + jnp.dot(up_grad, w_up.T, preferred_element_type=jnp.float32)
    scaled = normed_grad * norm_gain
    inner = lax.optimization_barrier(jnp.mean(scaled * embed_rows, axis=1, keepdims=True))
    result = out_grad + inv_rms * (scaled - embed_rows * inv_rms * inv_rms * inner)
    return result.astype(jnp.bfloat16)
```

```python
import math

import jax
import jax.numpy as jnp
from jax import lax
from jax.sharding import PartitionSpec as P

D = 8192
EPS = 1e-05
BF = jnp.bfloat16
F32 = jnp.float32
WIRE = BF


def contract_last(left, right):
    return lax.dot_general(left, right, (((1,), (1,)), ((), ())), preferred_element_type=F32)


def split_hi_lo(value):
    high = lax.reduce_precision(value, exponent_bits=8, mantissa_bits=7)
    return high.astype(BF), (value - high).astype(BF)


def swap(blocks):
    return lax.all_to_all(blocks, "wide", 0, 0, tiled=True)


def body(token_ids, attr_ids, target, loss_mask, embed_table, norm_gain, w_gate, w_up, w_down):
    wide = lax.axis_size("wide")
    narrow = lax.axis_size("narrow")
    my_wide = lax.axis_index("wide")
    my_narrow = lax.axis_index("narrow")
    tok_dev = token_ids.shape[0]
    tokens = tok_dev * wide
    attrs = attr_ids.shape[0]
    vocab_rows, cols = embed_table.shape
    ff = w_gate.shape[1]
    logit_scale = 3.0 / math.sqrt(D)

    def shift(step):
        return [(i, (i + step) % narrow) for i in range(narrow)]

    def rows_here(ids):
        local = jnp.clip(ids - my_wide * vocab_rows, 0, vocab_rows - 1)
        return jnp.take(embed_table, local, axis=0)

    def pick(received, ids):
        owner = ids // vocab_rows
        return jnp.concatenate(
            [
                lax.dynamic_slice(received, (owner[i], i, 0), (1, 1, cols)).reshape(1, cols)
                for i in range(tok_dev)
            ],
            axis=0,
        )

    ids_high = (token_ids // 256).astype(BF)
    ids_low = (token_ids % 256).astype(BF)
    extra = jnp.stack([ids_high, ids_low], axis=1)
    extra = jnp.pad(extra, ((0, 0), (0, 126)))
    probe_out = rows_here(attr_ids).reshape(wide, tok_dev, cols)
    first = jnp.concatenate(
        [probe_out, jnp.broadcast_to(extra[None], (wide, tok_dev, 128))], axis=2
    )
    first = swap(first)
    digits = first[:, :, cols : cols + 2].astype(F32)
    all_ids = (digits[:, :, 0] * 256.0 + digits[:, :, 1]).astype(jnp.int32).reshape(tokens)
    my_attrs = lax.dynamic_slice_in_dim(attr_ids, my_wide * tok_dev, tok_dev, 0)
    probe_own = pick(first, my_attrs)

    rows_out = rows_here(all_ids).reshape(wide, tok_dev, cols)
    second = swap(
        jnp.concatenate(
            [rows_out, jnp.broadcast_to(probe_own[None], (wide, tok_dev, cols))], axis=1
        )
    )
    probe = second[:, tok_dev:, :].reshape(attrs, cols)
    rows_own = pick(second, token_ids)
    rows = swap(jnp.broadcast_to(rows_own[None], (wide, tok_dev, cols))).reshape(tokens, cols)

    down_part = contract_last(w_down, probe).astype(WIRE)
    down_sum = down_part.astype(F32)
    for step in range(1, narrow):
        down_sum = down_sum + lax.ppermute(down_part, "narrow", shift(step)).astype(F32)
    down_high, down_low = split_hi_lo(down_sum)
    down_pair = jnp.concatenate([down_high, down_low], axis=1)

    own_high, own_low = split_hi_lo(contract_last(probe, rows_own))
    rows_f = rows.astype(F32)
    scaled_rows = (rows_f * norm_gain).astype(BF)
    gate_part = jnp.dot(scaled_rows, w_gate, preferred_element_type=F32)
    up_part = jnp.dot(scaled_rows, w_up, preferred_element_type=F32)
    sq_high, sq_low = split_hi_lo(jnp.sum(rows_f * rows_f, axis=1, keepdims=True))
    part = jnp.concatenate(
        [
            gate_part.astype(BF),
            up_part.astype(BF),
            sq_high,
            sq_low,
            own_high,
            own_low,
            jnp.zeros((tokens, 122), BF),
        ],
        axis=1,
    )
    summed = part.astype(F32)
    for step in range(1, narrow):
        summed = summed + lax.ppermute(part, "narrow", shift(step)).astype(F32)
    squares = summed[:, 2 * ff : 2 * ff + 1] + summed[:, 2 * ff + 1 : 2 * ff + 2]
    inv_all = lax.rsqrt(squares / D + EPS)
    gate_pre = summed[:, :ff] * inv_all
    up_pre = summed[:, ff : 2 * ff] * inv_all
    own_logits = (
        summed[:, 2 * ff + 2 : 2 * ff + 4] + summed[:, 2 * ff + 4 : 2 * ff + 6]
    ).T
    inv_own = lax.dynamic_slice_in_dim(inv_all, my_wide * tok_dev, tok_dev, 0)

    gate_sigmoid = jax.nn.sigmoid(gate_pre)
    hidden = (gate_pre * gate_sigmoid * up_pre).astype(BF)
    logit_pair = jnp.dot(hidden, down_pair, preferred_element_type=F32)
    logit_part = logit_pair[:, :attrs] + logit_pair[:, attrs:]
    logit_sum = jnp.sum(swap(logit_part.reshape(wide, tok_dev, attrs)), axis=0)
    logits = (logit_sum + own_logits) * logit_scale
    probability = jax.nn.softmax(logits, axis=1)
    onehot = (target[:, None] == jnp.arange(attrs, dtype=jnp.int32)[None, :]).astype(F32)
    grad_own = ((probability - onehot) * loss_mask[:, None].astype(F32)).astype(BF)
    logit_grad = swap(jnp.broadcast_to(grad_own[None], (wide, tok_dev, attrs))).reshape(
        tokens, attrs
    )
    out_grad = jnp.dot(grad_own, probe, preferred_element_type=F32)

    hidden_grad = contract_last(logit_grad, down_high)
    gate_grad = (
        hidden_grad * up_pre * gate_sigmoid * (1.0 + gate_pre * (1.0 - gate_sigmoid))
    ).astype(BF)
    up_grad = (hidden_grad * gate_pre * gate_sigmoid).astype(BF)
    inner_part = jnp.sum(
        gate_grad.astype(F32) * gate_pre + up_grad.astype(F32) * up_pre, axis=1, keepdims=True
    )
    inner_high, inner_low = split_hi_lo(inner_part)
    normed_part = contract_last(gate_grad, w_gate) + contract_last(up_grad, w_up)
    last = jnp.concatenate(
        [normed_part.astype(BF), inner_high, inner_low, jnp.zeros((tokens, 126), BF)], axis=1
    )
    last = swap(last.reshape(wide, tok_dev, cols + 128))
    last = jnp.sum(last.astype(F32), axis=0)
    scaled = last[:, :cols] * norm_gain
    inner = last[:, cols : cols + 1] + last[:, cols + 1 : cols + 2]
    result = out_grad + inv_own * scaled - rows_own.astype(F32) * (inv_own * inv_own * inner / D)
    return result.astype(BF)


def solution(mesh):
    return jax.shard_map(
        body,
        mesh=mesh,
        in_specs=(
            P("wide"),
            P(),
            P("wide"),
            P("wide"),
            P("wide", "narrow"),
            P("narrow"),
            P("narrow", "wide"),
            P("narrow", "wide"),
            P("wide", "narrow"),
        ),
        out_specs=P("wide", "narrow"),
        check_vma=False,
    )
```

```python
import functools
import math

import jax
import jax.numpy as jnp
from jax import lax
from jax.experimental import pallas as pl
from jax.experimental.pallas import tpu as pltpu
from jax.sharding import PartitionSpec as P

D = 8192
EPS = 1e-05
BF = jnp.bfloat16
F32 = jnp.float32


def contract_last(left, right):
    return lax.dot_general(left, right, (((1,), (1,)), ((), ())), preferred_element_type=F32)


def gather_kernel(cols, ids_ref, low_ref, table_ref, extra_ref, out_ref, held, found, sems):
    rows = table_ref.shape[0]
    count = ids_ref.shape[0]
    low = low_ref[0]

    total = jnp.int32(0)
    for i in range(count):
        local = ids_ref[i] - low
        found[total] = i
        total = total + ((local >= 0) & (local < rows)).astype(jnp.int32)

    def copy(k):
        local = jnp.clip(ids_ref[found[k]] - low, 0, rows - 1)
        start = pl.multiple_of(lax.shift_left(lax.shift_right_logical(local, 3), 3), 8)
        return pltpu.make_async_copy(table_ref.at[pl.ds(start, 8), :], held.at[k], sems.at[k])

    def begin(k, carry):
        copy(k).start()
        return carry

    lax.fori_loop(0, total, begin, 0)
    extra = extra_ref[...]
    if extra.shape[1] == cols:
        out_ref[:, 2:4, :] = jnp.broadcast_to(extra[None], (count // 2, 2, cols))
    else:
        out_ref[:, :, cols:] = jnp.broadcast_to(extra[None], (count // 2, 2, extra.shape[1]))

    def finish(k, carry):
        copy(k).wait()
        i = found[k]
        local = ids_ref[i] - low
        row = lax.broadcasted_iota(jnp.int32, (8, cols), 0)
        wanted = jnp.where(row == (local & 7), held[k].astype(F32), 0.0)
        wanted = jnp.sum(wanted, axis=0, keepdims=True)
        which = lax.broadcasted_iota(jnp.int32, (2, cols), 0)
        pair = lax.shift_right_logical(i, 1)
        before = out_ref[pair, 0:2, 0:cols].astype(F32)
        out_ref[pair, 0:2, 0:cols] = jnp.where(which == (i & 1), wanted, before).astype(BF)
        return carry

    lax.fori_loop(0, total, finish, 0)


def gather_rows(ids, low, table, extra):
    count, cols = ids.shape[0], table.shape[1]
    block = (4, cols) if extra.shape[1] == cols else (2, cols + extra.shape[1])
    smem = pl.BlockSpec(memory_space=pltpu.SMEM)
    vmem = pl.BlockSpec(memory_space=pltpu.VMEM)
    table = pltpu.with_memory_space_constraint(table, pltpu.HBM)
    args = (ids, low, table, extra)
    return pl.pallas_call(
        functools.partial(gather_kernel, cols),
        out_shape=jax.ShapeDtypeStruct((count // 2,) + block, BF),
        in_specs=[smem, smem, pl.BlockSpec(memory_space=pltpu.HBM), vmem],
        out_specs=vmem,
        scratch_shapes=[
            pltpu.VMEM((count, 8, cols), BF),
            pltpu.SMEM((count + 1,), jnp.int32),
            pltpu.SemaphoreType.DMA((count,)),
        ],
        compiler_params=pltpu.CompilerParams(vmem_limit_bytes=16 << 20),
        cost_estimate=pl.CostEstimate(flops=0, transcendentals=0, bytes_accessed=1 << 20),
    )(*args)


def column(row, size):
    shape = (size, size)
    same = lax.broadcasted_iota(jnp.int32, shape, 0) == lax.broadcasted_iota(jnp.int32, shape, 1)
    return jnp.sum(jnp.where(same, row, 0.0), axis=1, keepdims=True)


def row_of(col, size):
    shape = (size, size)
    same = lax.broadcasted_iota(jnp.int32, shape, 0) == lax.broadcasted_iota(jnp.int32, shape, 1)
    return jnp.sum(jnp.where(same, col, 0.0), axis=0, keepdims=True)


def halves(value):
    high = value.astype(BF).astype(F32)
    return high, value - high


def forward_kernel(rows_ref, gain_ref, weight_ref, own_ref, probe_ref, out_ref):
    cols = rows_ref.shape[2]
    tokens = rows_ref.shape[0] * rows_ref.shape[1]
    rows = rows_ref[...].reshape(tokens, cols).astype(F32)
    scaled = (rows * gain_ref[...]).astype(BF)
    out_ref[0:tokens, :] = contract_last(scaled, weight_ref[...]).astype(BF)
    squares = row_of(jnp.sum(rows * rows, axis=1, keepdims=True), tokens)
    sq_high, sq_low = halves(squares)
    own_high, own_low = halves(contract_last(own_ref[...], probe_ref[...]))
    at = lax.broadcasted_iota(jnp.int32, (8, tokens), 0)
    side = jnp.zeros((8, tokens), F32)
    lines = [sq_high, sq_low, own_high[0:1], own_high[1:2], own_low[0:1], own_low[1:2]]
    for i, line in enumerate(lines):
        side = jnp.where(at == i, line, side)
    out_ref[tokens:, 0:tokens] = side.astype(BF)
    out_ref[tokens:, tokens:] = jnp.zeros((8, out_ref.shape[1] - tokens), BF)


def middle_kernel(tokens, sums_ref, *rest):
    down_refs, (logit_ref, gate_up_ref, inv_ref, side_ref, down_ref) = rest[:-5], rest[-5:]
    block = tokens + 8
    total = sums_ref[0:block, :].astype(F32)
    for k in range(1, sums_ref.shape[0] // block):
        total = total + sums_ref[k * block : (k + 1) * block, :].astype(F32)
    side = total[tokens:, 0:tokens]
    side_ref[...] = side
    inv = lax.rsqrt(column(side[0:1] + side[1:2], tokens) / D + EPS)
    inv_ref[...] = jnp.broadcast_to(inv, (tokens, 128))
    gate_up = total[0:tokens] * inv
    gate_up_ref[...] = gate_up
    main = gate_up.shape[1] // 2 - 64
    gate, shared, up = gate_up[:, :main], gate_up[:, main : main + 128], gate_up[:, main + 128 :]
    hidden = gate * jax.nn.sigmoid(gate) * up
    lane = lax.broadcasted_iota(jnp.int32, shared.shape, 1)
    tail = jnp.where(lane < 64, shared * jax.nn.sigmoid(shared) * pltpu.roll(shared, 64, 1), 0.0)
    hidden = jnp.concatenate([hidden, tail], axis=1).astype(BF)
    down = down_refs[0][...].astype(F32)
    for ref in down_refs[1:]:
        down = down + ref[...].astype(F32)
    high, low = halves(down)
    down_ref[...] = high.astype(BF)
    pad = jnp.zeros((64, high.shape[1]), BF)
    high = jnp.concatenate([high.astype(BF), pad], axis=0)
    low = jnp.concatenate([low.astype(BF), pad], axis=0)
    logit_ref[...] = jnp.dot(hidden, high, preferred_element_type=F32) + jnp.dot(
        hidden, low, preferred_element_type=F32
    )


def backward_kernel(grad_ref, down_ref, gate_up_ref, weight_ref, out_ref):
    cols = weight_ref.shape[1]
    gate_up = gate_up_ref[...]
    main = gate_up.shape[1] // 2 - 64
    gate, shared, up = gate_up[:, :main], gate_up[:, main : main + 128], gate_up[:, main + 128 :]
    down = down_ref[...]
    down = jnp.concatenate([down, jnp.zeros((64, down.shape[1]), BF)], axis=0)
    hidden_grad = contract_last(grad_ref[...], down)

    def both(grad, gate, up):
        sig = jax.nn.sigmoid(gate)
        return grad * up * sig * (1.0 + gate * (1.0 - sig)), grad * gate * sig

    gate_grad, up_grad = both(hidden_grad[:, :main], gate, up)
    tail_gate, tail_up = both(hidden_grad[:, main:], shared, pltpu.roll(shared, 64, 1))
    lane = lax.broadcasted_iota(jnp.int32, shared.shape, 1)
    tail = jnp.where(lane < 64, tail_gate, pltpu.roll(tail_up, 64, 1))
    grads = jnp.concatenate([gate_grad, tail, up_grad], axis=1).astype(BF)
    normed = jnp.dot(grads, weight_ref[...], preferred_element_type=F32)
    shape = out_ref.shape[:2]
    out_ref[:, :, 0:cols] = normed.astype(BF).reshape(shape + (cols,))
    inner = jnp.sum(grads.astype(F32) * gate_up, axis=1, keepdims=True)
    high, low = halves(inner)
    pair = jnp.where(lane == 0, high, jnp.where(lane == 1, low, 0.0))
    out_ref[:, :, cols:] = pair.astype(BF).reshape(shape + (128,))


def on_core(kernel, out_shape, *args, flops=0):
    return pl.pallas_call(
        kernel,
        out_shape=out_shape,
        compiler_params=pltpu.CompilerParams(vmem_limit_bytes=24 << 20),
        cost_estimate=pl.CostEstimate(flops=flops, transcendentals=0, bytes_accessed=5 << 20),
    )(*args)


def swap(blocks):
    return lax.all_to_all(blocks, "wide", 0, 0, tiled=True)


def body(token_ids, attr_ids, target, loss_mask, embed_table, norm_gain, w_gate, w_up, w_down):
    wide = lax.axis_size("wide")
    narrow = lax.axis_size("narrow")
    my_wide = lax.axis_index("wide")
    tok_dev = token_ids.shape[0]
    tokens = tok_dev * wide
    attrs = attr_ids.shape[0]
    vocab_rows, cols = embed_table.shape
    ff = w_gate.shape[1]
    logit_scale = 3.0 / math.sqrt(D)

    def pick(received, ids):
        owner = ids // vocab_rows
        return jnp.concatenate(
            [
                lax.dynamic_slice(received, (owner[i], i, 0), (1, 1, cols)).reshape(1, cols)
                for i in range(tok_dev)
            ],
            axis=0,
        )

    main = ff // 128 * 128
    weight = jnp.concatenate([w_gate.T, w_up.T[main:], w_up.T[:main]], axis=0)

    ids_high = (token_ids // 256).astype(BF)
    ids_low = (token_ids % 256).astype(BF)
    extra = jnp.stack([ids_high, ids_low], axis=1)
    extra = jnp.pad(extra, ((0, 0), (0, 126)))
    low = (my_wide * vocab_rows).reshape(1)
    first = swap(gather_rows(attr_ids, low, embed_table, extra))
    digits = first[:, :, cols : cols + 2].astype(F32)
    all_ids = (digits[:, :, 0] * 256.0 + digits[:, :, 1]).astype(jnp.int32).reshape(tokens)
    my_attrs = lax.dynamic_slice_in_dim(attr_ids, my_wide * tok_dev, tok_dev, 0)
    probe_own, weight = lax.optimization_barrier((pick(first, my_attrs), weight))

    second = swap(gather_rows(all_ids, low, embed_table, probe_own))
    probe = second[:, tok_dev:, :].reshape(attrs, cols)
    rows_own = pick(second, token_ids)
    rows = swap(jnp.broadcast_to(rows_own[None], (wide, tok_dev, cols)))

    down_part = contract_last(w_down, probe).astype(BF)
    down_parts = [down_part]
    for step in range(1, narrow):
        pairs = [(i, (i + step) % narrow) for i in range(narrow)]
        down_parts.append(lax.ppermute(down_part, "narrow", pairs))

    part = on_core(
        forward_kernel,
        jax.ShapeDtypeStruct((tokens + 8, 2 * ff), BF),
        rows,
        norm_gain.reshape(1, cols),
        weight,
        rows_own,
        probe,
        flops=4 * tokens * cols * ff,
    )
    sums = lax.all_gather(part, "narrow", axis=0, tiled=True)
    logit_part, gate_up, inv_all, side, down_probe = on_core(
        functools.partial(middle_kernel, tokens),
        (
            jax.ShapeDtypeStruct((tokens, attrs), F32),
            jax.ShapeDtypeStruct((tokens, 2 * ff), F32),
            jax.ShapeDtypeStruct((tokens, 128), F32),
            jax.ShapeDtypeStruct((8, attrs), F32),
            jax.ShapeDtypeStruct((ff, attrs), BF),
        ),
        sums,
        *down_parts,
        flops=4 * tokens * ff * attrs,
    )
    own_logits = side[2:4] + side[4:6]
    inv_own = lax.dynamic_slice_in_dim(inv_all, my_wide * tok_dev, tok_dev, 0)[:, :1]

    logit_sum = jnp.sum(swap(logit_part.reshape(wide, tok_dev, attrs)), axis=0)
    logits = (logit_sum + own_logits) * logit_scale
    probability = jax.nn.softmax(logits, axis=1)
    onehot = (target[:, None] == jnp.arange(attrs, dtype=jnp.int32)[None, :]).astype(F32)
    grad_own = ((probability - onehot) * loss_mask[:, None].astype(F32)).astype(BF)
    logit_grad = swap(jnp.broadcast_to(grad_own[None], (wide, tok_dev, attrs))).reshape(
        tokens, attrs
    )
    out_grad = jnp.dot(grad_own, probe, preferred_element_type=F32)

    last = on_core(
        backward_kernel,
        jax.ShapeDtypeStruct((wide, tok_dev, cols + 128), BF),
        logit_grad,
        down_probe,
        gate_up,
        weight,
        flops=4 * tokens * cols * ff,
    )
    last = swap(last)
    last = jnp.sum(last.astype(F32), axis=0)
    scaled = last[:, :cols] * norm_gain
    inner = last[:, cols : cols + 1] + last[:, cols + 1 : cols + 2]
    result = out_grad + inv_own * scaled - rows_own.astype(F32) * (inv_own * inv_own * inner / D)
    return result.astype(BF)


def solution(mesh):
    return jax.shard_map(
        body,
        mesh=mesh,
        in_specs=(
            P("wide"),
            P(),
            P("wide"),
            P("wide"),
            P("wide", "narrow"),
            P("narrow"),
            P("narrow", "wide"),
            P("narrow", "wide"),
            P("wide", "narrow"),
        ),
        out_specs=P("wide", "narrow"),
        check_vma=False,
    )
```

```python
import functools
import math

import jax
import jax.numpy as jnp
from jax import lax
from jax.experimental import pallas as pl
from jax.experimental.pallas import tpu as pltpu
from jax.sharding import PartitionSpec as P

D = 8192
EPS = 1e-05
BF = jnp.bfloat16
F32 = jnp.float32


def contract_last(left, right):
    return lax.dot_general(left, right, (((1,), (1,)), ((), ())), preferred_element_type=F32)


def column(row, size):
    shape = (size, size)
    same = lax.broadcasted_iota(jnp.int32, shape, 0) == lax.broadcasted_iota(jnp.int32, shape, 1)
    return jnp.sum(jnp.where(same, row, 0.0), axis=1, keepdims=True)


def row_of(col, size):
    shape = (size, size)
    same = lax.broadcasted_iota(jnp.int32, shape, 0) == lax.broadcasted_iota(jnp.int32, shape, 1)
    return jnp.sum(jnp.where(same, col, 0.0), axis=0, keepdims=True)


def collect(ids, low, table_ref, out_ref, held, sems, meta_ref, meta_sem, list_ref):
    rows, cols = table_ref.shape
    count = ids.shape[0]
    local = ids - low.astype(F32)
    mine = jnp.where((local >= 0.0) & (local < float(rows)), 1.0, 0.0)
    at = lax.broadcasted_iota(jnp.int32, (count, count), 0)
    slot = lax.broadcasted_iota(jnp.int32, (count, count), 1)
    ahead = jnp.sum(jnp.where(slot < at, row_of(mine, count), 0.0), axis=1, keepdims=True)
    chosen = slot.astype(F32) == jnp.broadcast_to(jnp.where(mine > 0.0, ahead, -1.0), (count, count))
    which = jnp.sum(jnp.where(chosen, at.astype(F32), 0.0), axis=0, keepdims=True)
    place = jnp.sum(jnp.where(chosen, local, 0.0), axis=0, keepdims=True)
    total = jnp.sum(jnp.broadcast_to(mine, (count, count)), axis=0, keepdims=True)
    line = lax.broadcasted_iota(jnp.int32, (8, count), 0)
    meta = jnp.where(line == 0, which, jnp.where(line == 1, place, total))
    meta_ref[...] = meta.astype(jnp.int32)
    to_scalars = pltpu.make_async_copy(meta_ref, list_ref, meta_sem)
    to_scalars.start()
    to_scalars.wait()

    def copy(k):
        first = lax.shift_left(lax.shift_right_logical(list_ref[1, k], 3), 3)
        return pltpu.make_async_copy(
            table_ref.at[pl.ds(pl.multiple_of(first, 8), 8), :], held.at[k], sems.at[k]
        )

    def begin(k, carry):
        copy(k).start()
        return carry

    lax.fori_loop(0, list_ref[2, 0], begin, 0)

    def put(k, carry):
        copy(k).wait()
        i = list_ref[0, k]
        row = lax.broadcasted_iota(jnp.int32, (8, cols), 0)
        wanted = jnp.where(row == (list_ref[1, k] & 7), held[k].astype(F32), 0.0)
        wanted = jnp.sum(wanted, axis=0, keepdims=True)
        which = lax.broadcasted_iota(jnp.int32, (2, cols), 0)
        pair = lax.shift_right_logical(i, 1)
        before = out_ref[pair, 0:2, 0:cols].astype(F32)
        out_ref[pair, 0:2, 0:cols] = jnp.where(which == (i & 1), wanted, before).astype(BF)
        return carry

    return lambda: lax.fori_loop(0, list_ref[2, 0], put, 0)


def pick(blocks_ref, ids, cols):
    which = lax.broadcasted_iota(jnp.int32, (2, cols), 0)
    blocks = [blocks_ref[owner, 0:2, 0:cols].astype(F32) for owner in ids]
    return jnp.where(which == 0, blocks[0], blocks[1]).astype(BF)


def first_kernel(low_ref, token_ref, ids_ref, table_ref, out_ref, *scratch):
    cols = table_ref.shape[1]
    count = ids_ref.shape[1]
    ids = column(ids_ref[...].astype(F32), count)
    finish = collect(ids, low_ref[0], table_ref, out_ref, *scratch)
    which = lax.broadcasted_iota(jnp.int32, (2, 128), 0)
    lane = lax.broadcasted_iota(jnp.int32, (2, 128), 1)
    ids = jnp.where(which == 0, token_ref[0], token_ref[1])
    digits = jnp.where(lane == 0, lax.shift_right_logical(ids, 8), jnp.where(lane == 1, ids & 255, 0))
    digits = digits.astype(F32).astype(BF)
    out_ref[:, :, cols:] = jnp.broadcast_to(digits[None], (count // 2,) + digits.shape)
    finish()


def second_kernel(low_ref, attr_ref, first_ref, table_ref, out_ref, *scratch):
    rows, cols = table_ref.shape
    count = attr_ref.shape[0]
    low = low_ref[0]
    extra = first_ref[:, :, cols:].reshape(count, 128).astype(F32)
    lane = lax.broadcasted_iota(jnp.int32, (count, 128), 1)
    digits = jnp.where(lane == 0, extra * 256.0, jnp.where(lane == 1, extra, 0.0))
    ids = jnp.sum(digits, axis=1, keepdims=True)
    finish = collect(ids, low, table_ref, out_ref, *scratch)
    mine = 2 * lax.div(low, rows)
    own = pick(first_ref, [lax.div(attr_ref[mine + i], rows) for i in range(2)], cols)
    out_ref[:, 2:4, :] = jnp.broadcast_to(own[None], (count // 2, 2, cols))
    finish()


def on_table(kernel, block, low, scalars, values, table):
    count, cols = 2 * block[0], table.shape[1]
    table = pltpu.with_memory_space_constraint(table, pltpu.HBM)
    smem = pl.BlockSpec(memory_space=pltpu.SMEM)
    vmem = pl.BlockSpec(memory_space=pltpu.VMEM)
    return pl.pallas_call(
        kernel,
        out_shape=jax.ShapeDtypeStruct(block, BF),
        in_specs=[smem, smem, vmem, pl.BlockSpec(memory_space=pltpu.HBM)],
        out_specs=vmem,
        scratch_shapes=[
            pltpu.VMEM((count, 8, cols), BF),
            pltpu.SemaphoreType.DMA((count,)),
            pltpu.VMEM((8, count), jnp.int32),
            pltpu.SemaphoreType.DMA(()),
            pltpu.SMEM((8, count), jnp.int32),
        ],
        compiler_params=pltpu.CompilerParams(vmem_limit_bytes=16 << 20),
        cost_estimate=pl.CostEstimate(flops=0, transcendentals=0, bytes_accessed=1 << 20),
    )(low, scalars, values, table)


def own_kernel(ids_ref, rows_of_device, blocks_ref, own_ref, out_ref):
    cols = own_ref.shape[1]
    own = pick(blocks_ref, [lax.div(ids_ref[i], rows_of_device) for i in range(2)], cols)
    own_ref[...] = own
    out_ref[...] = jnp.broadcast_to(own[None], out_ref.shape)


def down_kernel(blocks_ref, own_ref, weight_ref, probe_ref, out_ref, logit_ref):
    probe = blocks_ref[:, 2:4, :].reshape(probe_ref.shape)
    probe_ref[...] = probe
    out_ref[...] = contract_last(weight_ref[...], probe).astype(BF)
    logit_ref[...] = contract_last(own_ref[...], probe)


def halves(value):
    high = value.astype(BF).astype(F32)
    return high, value - high


def weight_pieces(gate_ref, up_ref, held, sem):
    hidden = gate_ref.shape[0]
    main = hidden - 64
    copy = pltpu.make_async_copy(up_ref, held, sem)
    copy.start()

    def late():
        copy.wait()
        both = jnp.concatenate([gate_ref[main:, :], held[main:, :]], axis=0)
        return [(main, main + 128, both), (main + 128, 2 * hidden, held[:main, :])]

    return (0, main, gate_ref[:main, :]), late


def forward_kernel(rows_ref, gain_ref, own_ref, gate_ref, up_ref, out_ref, held, sem):
    piece, late = weight_pieces(gate_ref, up_ref, held, sem)
    cols = rows_ref.shape[2]
    tokens = rows_ref.shape[0] * rows_ref.shape[1]
    rows = rows_ref[...].reshape(tokens, cols).astype(F32)
    scaled = (rows * gain_ref[...]).astype(BF)
    squares = row_of(jnp.sum(rows * rows, axis=1, keepdims=True), tokens)
    sq_high, sq_low = halves(squares)
    own_high, own_low = halves(own_ref[...])
    at = lax.broadcasted_iota(jnp.int32, (8, tokens), 0)
    side = jnp.zeros((8, tokens), F32)
    lines = [sq_high, sq_low, own_high[0:1], own_high[1:2], own_low[0:1], own_low[1:2]]
    for i, line in enumerate(lines):
        side = jnp.where(at == i, line, side)
    out_ref[tokens:, 0:tokens] = side.astype(BF)
    out_ref[tokens:, tokens:] = jnp.zeros((8, out_ref.shape[1] - tokens), BF)
    low, high, weight = piece
    out_ref[0:tokens, low:high] = contract_last(scaled, weight).astype(BF)
    for low, high, weight in late():
        out_ref[0:tokens, low:high] = contract_last(scaled, weight).astype(BF)


def middle_kernel(tokens, sums_ref, *rest):
    down_refs, (logit_ref, gate_up_ref, inv_ref, side_ref, down_ref) = rest[:-5], rest[-5:]
    block = tokens + 8
    total = sums_ref[0:block, :].astype(F32)
    for k in range(1, sums_ref.shape[0] // block):
        total = total + sums_ref[k * block : (k + 1) * block, :].astype(F32)
    side = total[tokens:, 0:tokens]
    side_ref[...] = side
    inv = lax.rsqrt(column(side[0:1] + side[1:2], tokens) / D + EPS)
    inv_ref[...] = jnp.broadcast_to(inv, (tokens, 128))
    gate_up = total[0:tokens] * inv
    gate_up_ref[...] = gate_up
    main = gate_up.shape[1] // 2 - 64
    gate, shared, up = gate_up[:, :main], gate_up[:, main : main + 128], gate_up[:, main + 128 :]
    hidden = gate * jax.nn.sigmoid(gate) * up
    lane = lax.broadcasted_iota(jnp.int32, shared.shape, 1)
    tail = jnp.where(lane < 64, shared * jax.nn.sigmoid(shared) * pltpu.roll(shared, 64, 1), 0.0)
    hidden = jnp.concatenate([hidden, tail], axis=1).astype(BF)
    down = down_refs[0][...].astype(F32)
    for ref in down_refs[1:]:
        down = down + ref[...].astype(F32)
    high, low = halves(down)
    down_ref[...] = high.astype(BF)
    pad = jnp.zeros((64, high.shape[1]), BF)
    high = jnp.concatenate([high.astype(BF), pad], axis=0)
    low = jnp.concatenate([low.astype(BF), pad], axis=0)
    logit_ref[...] = jnp.dot(hidden, high, preferred_element_type=F32) + jnp.dot(
        hidden, low, preferred_element_type=F32
    )


def backward_kernel(grad_ref, down_ref, gate_up_ref, gate_ref, up_ref, out_ref, held, sem):
    piece, late = weight_pieces(gate_ref, up_ref, held, sem)
    cols = gate_ref.shape[1]
    gate_up = gate_up_ref[...]
    main = gate_up.shape[1] // 2 - 64
    gate, shared, up = gate_up[:, :main], gate_up[:, main : main + 128], gate_up[:, main + 128 :]
    down = down_ref[...]
    down = jnp.concatenate([down, jnp.zeros((64, down.shape[1]), BF)], axis=0)
    hidden_grad = contract_last(grad_ref[...], down)

    def both(grad, gate, up):
        sig = jax.nn.sigmoid(gate)
        return grad * up * sig * (1.0 + gate * (1.0 - sig)), grad * gate * sig

    gate_grad, up_grad = both(hidden_grad[:, :main], gate, up)
    tail_gate, tail_up = both(hidden_grad[:, main:], shared, pltpu.roll(shared, 64, 1))
    lane = lax.broadcasted_iota(jnp.int32, shared.shape, 1)
    tail = jnp.where(lane < 64, tail_gate, pltpu.roll(tail_up, 64, 1))
    grads = jnp.concatenate([gate_grad, tail, up_grad], axis=1).astype(BF)
    low, high, weight = piece
    normed = jnp.dot(grads[:, low:high], weight, preferred_element_type=F32)
    for low, high, weight in late():
        normed = normed + jnp.dot(grads[:, low:high], weight, preferred_element_type=F32)
    shape = out_ref.shape[:2]
    out_ref[:, :, 0:cols] = normed.astype(BF).reshape(shape + (cols,))
    inner = jnp.sum(grads.astype(F32) * gate_up, axis=1, keepdims=True)
    high, low = halves(inner)
    pair = jnp.where(lane == 0, high, jnp.where(lane == 1, low, 0.0))
    out_ref[:, :, cols:] = pair.astype(BF).reshape(shape + (128,))


def on_core(kernel, out_shape, *args, scalars=(), late=None, flops=0):
    vmem = pl.BlockSpec(memory_space=pltpu.VMEM)
    in_specs = [pl.BlockSpec(memory_space=pltpu.SMEM) for _ in scalars] + [vmem for _ in args]
    scratch = []
    if late is not None:
        args = args + (pltpu.with_memory_space_constraint(late, pltpu.HBM),)
        in_specs.append(pl.BlockSpec(memory_space=pltpu.HBM))
        scratch = [pltpu.VMEM(late.shape, late.dtype), pltpu.SemaphoreType.DMA(())]
    return pl.pallas_call(
        kernel,
        out_shape=out_shape,
        in_specs=in_specs,
        out_specs=jax.tree.map(lambda _: vmem, out_shape),
        scratch_shapes=scratch,
        compiler_params=pltpu.CompilerParams(vmem_limit_bytes=16 << 20),
        cost_estimate=pl.CostEstimate(flops=flops, transcendentals=0, bytes_accessed=5 << 20),
    )(*scalars, *args)


def swap(blocks):
    return lax.all_to_all(blocks, "wide", 0, 0, tiled=True)


def body(token_ids, attr_ids, target, loss_mask, embed_table, norm_gain, w_gate, w_up, w_down):
    wide = lax.axis_size("wide")
    narrow = lax.axis_size("narrow")
    my_wide = lax.axis_index("wide")
    tok_dev = token_ids.shape[0]
    tokens = tok_dev * wide
    attrs = attr_ids.shape[0]
    vocab_rows, cols = embed_table.shape
    ff = w_gate.shape[1]
    logit_scale = 3.0 / math.sqrt(D)

    low = (my_wide * vocab_rows).reshape(1)
    first = swap(
        on_table(
            first_kernel,
            (wide, tok_dev, cols + 128),
            low,
            token_ids,
            attr_ids.reshape(1, attrs),
            embed_table,
        )
    )
    second = swap(
        on_table(second_kernel, (wide, 2 * tok_dev, cols), low, attr_ids, first, embed_table)
    )
    rows_own, rows = on_core(
        lambda ids, *refs: own_kernel(ids, vocab_rows, *refs),
        (
            jax.ShapeDtypeStruct((tok_dev, cols), BF),
            jax.ShapeDtypeStruct((wide, tok_dev, cols), BF),
        ),
        second,
        scalars=(token_ids,),
    )
    rows = swap(rows)

    probe, down_part, own_part = on_core(
        down_kernel,
        (
            jax.ShapeDtypeStruct((attrs, cols), BF),
            jax.ShapeDtypeStruct((ff, attrs), BF),
            jax.ShapeDtypeStruct((tok_dev, attrs), F32),
        ),
        second,
        rows_own,
        w_down,
        flops=2 * attrs * cols * ff,
    )
    down_parts = [down_part]
    for step in range(1, narrow):
        pairs = [(i, (i + step) % narrow) for i in range(narrow)]
        down_parts.append(lax.ppermute(down_part, "narrow", pairs))

    part = on_core(
        forward_kernel,
        jax.ShapeDtypeStruct((tokens + 8, 2 * ff), BF),
        rows,
        norm_gain.reshape(1, cols),
        own_part,
        w_gate.T,
        late=w_up.T,
        flops=4 * tokens * cols * ff,
    )
    sums = lax.all_gather(part, "narrow", axis=0, tiled=True)
    logit_part, gate_up, inv_all, side, down_probe = on_core(
        functools.partial(middle_kernel, tokens),
        (
            jax.ShapeDtypeStruct((tokens, attrs), F32),
            jax.ShapeDtypeStruct((tokens, 2 * ff), F32),
            jax.ShapeDtypeStruct((tokens, 128), F32),
            jax.ShapeDtypeStruct((8, attrs), F32),
            jax.ShapeDtypeStruct((ff, attrs), BF),
        ),
        sums,
        *down_parts,
        flops=4 * tokens * ff * attrs,
    )
    own_logits = side[2:4] + side[4:6]
    inv_own = lax.dynamic_slice_in_dim(inv_all, my_wide * tok_dev, tok_dev, 0)[:, :1]

    logit_sum = jnp.sum(swap(logit_part.reshape(wide, tok_dev, attrs)), axis=0)
    logits = (logit_sum + own_logits) * logit_scale
    probability = jax.nn.softmax(logits, axis=1)
    onehot = (target[:, None] == jnp.arange(attrs, dtype=jnp.int32)[None, :]).astype(F32)
    grad_own = ((probability - onehot) * loss_mask[:, None].astype(F32)).astype(BF)
    logit_grad = swap(jnp.broadcast_to(grad_own[None], (wide, tok_dev, attrs))).reshape(
        tokens, attrs
    )
    out_grad = jnp.dot(grad_own, probe, preferred_element_type=F32)

    last = on_core(
        backward_kernel,
        jax.ShapeDtypeStruct((wide, tok_dev, cols + 128), BF),
        logit_grad,
        down_probe,
        gate_up,
        w_gate.T,
        late=w_up.T,
        flops=4 * tokens * cols * ff,
    )
    last, out_grad = lax.optimization_barrier((swap(last), out_grad))
    last = jnp.sum(last.astype(F32), axis=0)
    scaled = last[:, :cols] * norm_gain
    inner = last[:, cols : cols + 1] + last[:, cols + 1 : cols + 2]
    result = out_grad + inv_own * scaled - rows_own.astype(F32) * (inv_own * inv_own * inner / D)
    return result.astype(BF)


def solution(mesh):
    return jax.shard_map(
        body,
        mesh=mesh,
        in_specs=(
            P("wide"),
            P(),
            P("wide"),
            P("wide"),
            P("wide", "narrow"),
            P("narrow"),
            P("narrow", "wide"),
            P("narrow", "wide"),
            P("wide", "narrow"),
        ),
        out_specs=P("wide", "narrow"),
        check_vma=False,
    )
```

```python
import functools
import math

import jax
import jax.numpy as jnp
from jax import lax
from jax.experimental import pallas as pl
from jax.experimental.pallas import tpu as pltpu
from jax.sharding import PartitionSpec as P

D = 8192
EPS = 1e-05
BF = jnp.bfloat16
F32 = jnp.float32


def contract_last(left, right):
    return lax.dot_general(left, right, (((1,), (1,)), ((), ())), preferred_element_type=F32)


def column(row, size):
    shape = (size, size)
    same = lax.broadcasted_iota(jnp.int32, shape, 0) == lax.broadcasted_iota(jnp.int32, shape, 1)
    return jnp.sum(jnp.where(same, row, 0.0), axis=1, keepdims=True)


def row_of(col, size):
    shape = (size, size)
    same = lax.broadcasted_iota(jnp.int32, shape, 0) == lax.broadcasted_iota(jnp.int32, shape, 1)
    return jnp.sum(jnp.where(same, col, 0.0), axis=0, keepdims=True)


def collect(ids, low, table_ref, out_ref, held, sems, meta_ref, meta_sem, list_ref):
    rows, cols = table_ref.shape
    count = ids.shape[0]
    local = ids - low.astype(F32)
    mine = jnp.where((local >= 0.0) & (local < float(rows)), 1.0, 0.0)
    at = lax.broadcasted_iota(jnp.int32, (count, count), 0)
    slot = lax.broadcasted_iota(jnp.int32, (count, count), 1)
    ahead = jnp.sum(jnp.where(slot < at, row_of(mine, count), 0.0), axis=1, keepdims=True)
    chosen = slot.astype(F32) == jnp.broadcast_to(jnp.where(mine > 0.0, ahead, -1.0), (count, count))
    which = jnp.sum(jnp.where(chosen, at.astype(F32), 0.0), axis=0, keepdims=True)
    place = jnp.sum(jnp.where(chosen, local, 0.0), axis=0, keepdims=True)
    total = jnp.sum(jnp.broadcast_to(mine, (count, count)), axis=0, keepdims=True)
    line = lax.broadcasted_iota(jnp.int32, (8, count), 0)
    meta = jnp.where(line == 0, which, jnp.where(line == 1, place, total))
    meta_ref[...] = meta.astype(jnp.int32)
    to_scalars = pltpu.make_async_copy(meta_ref, list_ref, meta_sem)
    to_scalars.start()
    to_scalars.wait()

    def copy(k):
        first = lax.shift_left(lax.shift_right_logical(list_ref[1, k], 3), 3)
        return pltpu.make_async_copy(
            table_ref.at[pl.ds(pl.multiple_of(first, 8), 8), :], held.at[k], sems.at[k]
        )

    def begin(k, carry):
        copy(k).start()
        return carry

    lax.fori_loop(0, list_ref[2, 0], begin, 0)

    def put(k, carry):
        copy(k).wait()
        i = list_ref[0, k]
        row = lax.broadcasted_iota(jnp.int32, (8, cols), 0)
        wanted = jnp.where(row == (list_ref[1, k] & 7), held[k].astype(F32), 0.0)
        wanted = jnp.sum(wanted, axis=0, keepdims=True)
        which = lax.broadcasted_iota(jnp.int32, (2, cols), 0)
        pair = lax.shift_right_logical(i, 1)
        before = out_ref[pair, 0:2, 0:cols].astype(F32)
        out_ref[pair, 0:2, 0:cols] = jnp.where(which == (i & 1), wanted, before).astype(BF)
        return carry

    return lambda: lax.fori_loop(0, list_ref[2, 0], put, 0)


def collect_listed(ids, low, table_ref, out_ref, held, found, sems, count):
    rows, cols = table_ref.shape
    total = jnp.int32(0)
    for i in range(count):
        local = ids(i) - low
        found[total] = i
        total = total + ((local >= 0) & (local < rows)).astype(jnp.int32)

    def copy(k):
        local = jnp.clip(ids(found[k]) - low, 0, rows - 1)
        start = pl.multiple_of(lax.shift_left(lax.shift_right_logical(local, 3), 3), 8)
        return pltpu.make_async_copy(table_ref.at[pl.ds(start, 8), :], held.at[k], sems.at[k])

    def begin(k, carry):
        copy(k).start()
        return carry

    lax.fori_loop(0, total, begin, 0)

    def place(k, carry):
        copy(k).wait()
        i = found[k]
        row = lax.broadcasted_iota(jnp.int32, (8, cols), 0)
        wanted = jnp.where(row == ((ids(i) - low) & 7), held[k].astype(F32), 0.0)
        wanted = jnp.sum(wanted, axis=0, keepdims=True)
        which = lax.broadcasted_iota(jnp.int32, (2, cols), 0)
        pair = lax.shift_right_logical(i, 1)
        before = out_ref[pair, 0:2, 0:cols].astype(F32)
        out_ref[pair, 0:2, 0:cols] = jnp.where(which == (i & 1), wanted, before).astype(BF)
        return carry

    return lambda: lax.fori_loop(0, total, place, 0)


def pick(blocks_ref, ids, cols):
    which = lax.broadcasted_iota(jnp.int32, (2, cols), 0)
    blocks = [blocks_ref[owner, 0:2, 0:cols].astype(F32) for owner in ids]
    return jnp.where(which == 0, blocks[0], blocks[1]).astype(BF)


def first_kernel(low_ref, token_ref, ids_ref, table_ref, out_ref, held, sems, *found):
    cols = table_ref.shape[1]
    count = ids_ref.shape[0]
    finish = collect_listed(
        lambda i: ids_ref[i], low_ref[0], table_ref, out_ref, held, found[0], sems, count
    )
    which = lax.broadcasted_iota(jnp.int32, (2, 128), 0)
    lane = lax.broadcasted_iota(jnp.int32, (2, 128), 1)
    ids = jnp.where(which == 0, token_ref[0], token_ref[1])
    digits = jnp.where(lane == 0, lax.shift_right_logical(ids, 8), jnp.where(lane == 1, ids & 255, 0))
    digits = digits.astype(F32).astype(BF)
    out_ref[:, :, cols:] = jnp.broadcast_to(digits[None], (count // 2,) + digits.shape)
    finish()


def second_kernel(low_ref, attr_ref, first_ref, table_ref, out_ref, *scratch):
    rows, cols = table_ref.shape
    count = attr_ref.shape[0]
    low = low_ref[0]
    extra = first_ref[:, :, cols:].reshape(count, 128).astype(F32)
    lane = lax.broadcasted_iota(jnp.int32, (count, 128), 1)
    digits = jnp.where(lane == 0, extra * 256.0, jnp.where(lane == 1, extra, 0.0))
    ids = jnp.sum(digits, axis=1, keepdims=True)
    finish = collect(ids, low, table_ref, out_ref, *scratch)
    mine = 2 * lax.div(low, rows)
    own = pick(first_ref, [lax.div(attr_ref[mine + i], rows) for i in range(2)], cols)
    out_ref[:, 2:4, :] = jnp.broadcast_to(own[None], (count // 2, 2, cols))
    finish()


def on_table(kernel, block, low, scalars, values, table):
    count, cols = 2 * block[0], table.shape[1]
    table = pltpu.with_memory_space_constraint(table, pltpu.HBM)
    smem = pl.BlockSpec(memory_space=pltpu.SMEM)
    vmem = pl.BlockSpec(memory_space=pltpu.VMEM)
    return pl.pallas_call(
        kernel,
        out_shape=jax.ShapeDtypeStruct(block, BF),
        in_specs=[
            smem,
            smem,
            smem if values.ndim == 1 else vmem,
            pl.BlockSpec(memory_space=pltpu.HBM),
        ],
        out_specs=vmem,
        scratch_shapes=[
            pltpu.VMEM((count, 8, cols), BF),
            pltpu.SemaphoreType.DMA((count,)),
            *(
                [pltpu.SMEM((count + 1,), jnp.int32)]
                if values.ndim == 1
                else [
                    pltpu.VMEM((8, count), jnp.int32),
                    pltpu.SemaphoreType.DMA(()),
                    pltpu.SMEM((8, count), jnp.int32),
                ]
            ),
        ],
        compiler_params=pltpu.CompilerParams(vmem_limit_bytes=16 << 20),
        cost_estimate=pl.CostEstimate(flops=0, transcendentals=0, bytes_accessed=1 << 20),
    )(low, scalars, values, table)


def own_kernel(ids_ref, rows_of_device, blocks_ref, own_ref, out_ref):
    cols = own_ref.shape[1]
    own = pick(blocks_ref, [lax.div(ids_ref[i], rows_of_device) for i in range(2)], cols)
    own_ref[...] = own
    out_ref[...] = jnp.broadcast_to(own[None], out_ref.shape)


def down_kernel(blocks_ref, own_ref, weight_ref, probe_ref, out_ref, logit_ref):
    probe = blocks_ref[:, 2:4, :].reshape(probe_ref.shape)
    probe_ref[...] = probe
    out_ref[...] = contract_last(weight_ref[...], probe).astype(BF)
    logit_ref[...] = contract_last(own_ref[...], probe)


def halves(value):
    high = value.astype(BF).astype(F32)
    return high, value - high


def weight_pieces(gate_ref, up_ref, held, sem):
    hidden = gate_ref.shape[0]
    main = hidden - 64
    copy = pltpu.make_async_copy(up_ref, held, sem)
    copy.start()

    def late():
        copy.wait()
        both = jnp.concatenate([gate_ref[main:, :], held[main:, :]], axis=0)
        return [(main, main + 128, both), (main + 128, 2 * hidden, held[:main, :])]

    return (0, main, gate_ref[:main, :]), late


def forward_kernel(rows_ref, gain_ref, own_ref, gate_ref, up_ref, out_ref, held, sem):
    piece, late = weight_pieces(gate_ref, up_ref, held, sem)
    cols = rows_ref.shape[2]
    tokens = rows_ref.shape[0] * rows_ref.shape[1]
    rows = rows_ref[...].reshape(tokens, cols).astype(F32)
    scaled = (rows * gain_ref[...]).astype(BF)
    squares = row_of(jnp.sum(rows * rows, axis=1, keepdims=True), tokens)
    sq_high, sq_low = halves(squares)
    own_high, own_low = halves(own_ref[...])
    at = lax.broadcasted_iota(jnp.int32, (8, tokens), 0)
    side = jnp.zeros((8, tokens), F32)
    lines = [sq_high, sq_low, own_high[0:1], own_high[1:2], own_low[0:1], own_low[1:2]]
    for i, line in enumerate(lines):
        side = jnp.where(at == i, line, side)
    out_ref[tokens:, 0:tokens] = side.astype(BF)
    out_ref[tokens:, tokens:] = jnp.zeros((8, out_ref.shape[1] - tokens), BF)
    low, high, weight = piece
    out_ref[0:tokens, low:high] = contract_last(scaled, weight).astype(BF)
    for low, high, weight in late():
        out_ref[0:tokens, low:high] = contract_last(scaled, weight).astype(BF)


def middle_kernel(tokens, sums_ref, *rest):
    down_refs, (logit_ref, gate_up_ref, inv_ref, side_ref, down_ref) = rest[:-5], rest[-5:]
    block = tokens + 8
    total = sums_ref[0:block, :].astype(F32)
    for k in range(1, sums_ref.shape[0] // block):
        total = total + sums_ref[k * block : (k + 1) * block, :].astype(F32)
    side = total[tokens:, 0:tokens]
    side_ref[...] = side
    inv = lax.rsqrt(column(side[0:1] + side[1:2], tokens) / D + EPS)
    inv_ref[...] = jnp.broadcast_to(inv, (tokens, 128))
    gate_up = total[0:tokens] * inv
    gate_up_ref[...] = gate_up
    main = gate_up.shape[1] // 2 - 64
    gate, shared, up = gate_up[:, :main], gate_up[:, main : main + 128], gate_up[:, main + 128 :]
    hidden = gate * jax.nn.sigmoid(gate) * up
    lane = lax.broadcasted_iota(jnp.int32, shared.shape, 1)
    tail = jnp.where(lane < 64, shared * jax.nn.sigmoid(shared) * pltpu.roll(shared, 64, 1), 0.0)
    hidden = jnp.concatenate([hidden, tail], axis=1).astype(BF)
    down = down_refs[0][...].astype(F32)
    for ref in down_refs[1:]:
        down = down + ref[...].astype(F32)
    high, low = halves(down)
    down_ref[...] = high.astype(BF)
    pad = jnp.zeros((64, high.shape[1]), BF)
    high = jnp.concatenate([high.astype(BF), pad], axis=0)
    low = jnp.concatenate([low.astype(BF), pad], axis=0)
    logit_ref[...] = jnp.dot(hidden, high, preferred_element_type=F32) + jnp.dot(
        hidden, low, preferred_element_type=F32
    )


def backward_kernel(
    core_ref, grad_ref, down_ref, gate_up_ref, gate_ref, up_ref, mine_ref, other_ref, held, sem
):
    piece, late = weight_pieces(gate_ref, up_ref, held, sem)
    cols = gate_ref.shape[1]
    gate_up = gate_up_ref[...]
    main = gate_up.shape[1] // 2 - 64
    gate, shared, up = gate_up[:, :main], gate_up[:, main : main + 128], gate_up[:, main + 128 :]
    down = down_ref[...]
    down = jnp.concatenate([down, jnp.zeros((64, down.shape[1]), BF)], axis=0)
    hidden_grad = contract_last(grad_ref[...], down)

    def both(grad, gate, up):
        sig = jax.nn.sigmoid(gate)
        return grad * up * sig * (1.0 + gate * (1.0 - sig)), grad * gate * sig

    gate_grad, up_grad = both(hidden_grad[:, :main], gate, up)
    tail_gate, tail_up = both(hidden_grad[:, main:], shared, pltpu.roll(shared, 64, 1))
    lane = lax.broadcasted_iota(jnp.int32, shared.shape, 1)
    tail = jnp.where(lane < 64, tail_gate, pltpu.roll(tail_up, 64, 1))
    grads = jnp.concatenate([gate_grad, tail, up_grad], axis=1).astype(BF)
    low, high, weight = piece
    normed = jnp.dot(grads[:, low:high], weight, preferred_element_type=F32)
    for low, high, weight in late():
        normed = normed + jnp.dot(grads[:, low:high], weight, preferred_element_type=F32)
    inner = jnp.sum(grads.astype(F32) * gate_up, axis=1, keepdims=True)
    high, low = halves(inner)
    pair = jnp.where(lane == 0, high, jnp.where(lane == 1, low, 0.0))
    chips = mine_ref.shape[0]
    first = core_ref[0] == 0
    for start, value in ((0, normed), (cols, pair)):
        width = value.shape[1]
        value = value.astype(BF).reshape(chips, 2, 2, width)
        even, odd = value[:, 0].astype(F32), value[:, 1].astype(F32)
        mine_ref[:, :, start : start + width] = jnp.where(first, even, odd).astype(BF)
        other_ref[:, :, start : start + width] = jnp.where(first, odd, even).astype(BF)


def on_core(kernel, out_shape, *args, scalars=(), late=None, flops=0):
    vmem = pl.BlockSpec(memory_space=pltpu.VMEM)
    in_specs = [pl.BlockSpec(memory_space=pltpu.SMEM) for _ in scalars] + [vmem for _ in args]
    scratch = []
    if late is not None:
        args = args + (pltpu.with_memory_space_constraint(late, pltpu.HBM),)
        in_specs.append(pl.BlockSpec(memory_space=pltpu.HBM))
        scratch = [pltpu.VMEM(late.shape, late.dtype), pltpu.SemaphoreType.DMA(())]
    return pl.pallas_call(
        kernel,
        out_shape=out_shape,
        in_specs=in_specs,
        out_specs=jax.tree.map(lambda _: vmem, out_shape),
        scratch_shapes=scratch,
        compiler_params=pltpu.CompilerParams(vmem_limit_bytes=16 << 20),
        cost_estimate=pl.CostEstimate(flops=flops, transcendentals=0, bytes_accessed=5 << 20),
    )(*scalars, *args)


def swap(blocks):
    return lax.all_to_all(blocks, "wide", 0, 0, tiled=True)


def body(token_ids, attr_ids, target, loss_mask, embed_table, norm_gain, w_gate, w_up, w_down):
    wide = lax.axis_size("wide")
    narrow = lax.axis_size("narrow")
    my_wide = lax.axis_index("wide")
    tok_dev = token_ids.shape[0]
    tokens = tok_dev * wide
    attrs = attr_ids.shape[0]
    vocab_rows, cols = embed_table.shape
    ff = w_gate.shape[1]
    logit_scale = 3.0 / math.sqrt(D)

    low = (my_wide * vocab_rows).reshape(1)
    first = swap(
        on_table(
            first_kernel,
            (wide, tok_dev, cols + 128),
            low,
            token_ids,
            attr_ids,
            embed_table,
        )
    )
    second = swap(
        on_table(second_kernel, (wide, 2 * tok_dev, cols), low, attr_ids, first, embed_table)
    )
    rows_own, rows = on_core(
        lambda ids, *refs: own_kernel(ids, vocab_rows, *refs),
        (
            jax.ShapeDtypeStruct((tok_dev, cols), BF),
            jax.ShapeDtypeStruct((wide, tok_dev, cols), BF),
        ),
        second,
        scalars=(token_ids,),
    )
    rows = swap(rows)

    probe, down_part, own_part = on_core(
        down_kernel,
        (
            jax.ShapeDtypeStruct((attrs, cols), BF),
            jax.ShapeDtypeStruct((ff, attrs), BF),
            jax.ShapeDtypeStruct((tok_dev, attrs), F32),
        ),
        second,
        rows_own,
        w_down,
        flops=2 * attrs * cols * ff,
    )
    down_parts = [down_part]
    for step in range(1, narrow):
        pairs = [(i, (i + step) % narrow) for i in range(narrow)]
        down_parts.append(lax.ppermute(down_part, "narrow", pairs))

    part = on_core(
        forward_kernel,
        jax.ShapeDtypeStruct((tokens + 8, 2 * ff), BF),
        rows,
        norm_gain.reshape(1, cols),
        own_part,
        w_gate.T,
        late=w_up.T,
        flops=4 * tokens * cols * ff,
    )
    sums = lax.all_gather(part, "narrow", axis=0, tiled=True)
    logit_part, gate_up, inv_all, side, down_probe = on_core(
        functools.partial(middle_kernel, tokens),
        (
            jax.ShapeDtypeStruct((tokens, attrs), F32),
            jax.ShapeDtypeStruct((tokens, 2 * ff), F32),
            jax.ShapeDtypeStruct((tokens, 128), F32),
            jax.ShapeDtypeStruct((8, attrs), F32),
            jax.ShapeDtypeStruct((ff, attrs), BF),
        ),
        sums,
        *down_parts,
        flops=4 * tokens * ff * attrs,
    )
    own_logits = side[2:4] + side[4:6]
    inv_own = lax.dynamic_slice_in_dim(inv_all, my_wide * tok_dev, tok_dev, 0)[:, :1]

    logit_sum = jnp.sum(swap(logit_part.reshape(wide, tok_dev, attrs)), axis=0)
    logits = (logit_sum + own_logits) * logit_scale
    probability = jax.nn.softmax(logits, axis=1)
    onehot = (target[:, None] == jnp.arange(attrs, dtype=jnp.int32)[None, :]).astype(F32)
    grad_own = ((probability - onehot) * loss_mask[:, None].astype(F32)).astype(BF)
    logit_grad = swap(jnp.broadcast_to(grad_own[None], (wide, tok_dev, attrs))).reshape(
        tokens, attrs
    )
    out_grad = jnp.dot(grad_own, probe, preferred_element_type=F32)

    half = jax.ShapeDtypeStruct((wide // 2, tok_dev, cols + 128), BF)
    mine, other = on_core(
        backward_kernel,
        (half, half),
        logit_grad,
        down_probe,
        gate_up,
        w_gate.T,
        late=w_up.T,
        scalars=((my_wide % 2).reshape(1),),
        flops=4 * tokens * cols * ff,
    )
    got = lax.ppermute(other, "wide", [(i, i ^ 1) for i in range(wide)])
    last = (mine.astype(F32) + got.astype(F32)).astype(BF)
    cores = [list(range(core, wide, 2)) for core in range(2)]
    last = lax.all_to_all(last, "wide", 0, 0, tiled=True, axis_index_groups=cores)
    last, out_grad = lax.optimization_barrier((last, out_grad))
    last = jnp.sum(last.astype(F32), axis=0)
    scaled = last[:, :cols] * norm_gain
    inner = last[:, cols : cols + 1] + last[:, cols + 1 : cols + 2]
    result = out_grad + inv_own * scaled - rows_own.astype(F32) * (inv_own * inv_own * inner / D)
    return result.astype(BF)


def solution(mesh):
    return jax.shard_map(
        body,
        mesh=mesh,
        in_specs=(
            P("wide"),
            P(),
            P("wide"),
            P("wide"),
            P("wide", "narrow"),
            P("narrow"),
            P("narrow", "wide"),
            P("narrow", "wide"),
            P("wide", "narrow"),
        ),
        out_specs=P("wide", "narrow"),
        check_vma=False,
    )
```
